768 devices in a mesh: dp: 64 (over y, x, core), pipe: 12 (over z).
Axes of the slice: x: 4, y: 8, z: 12, core: 2. Of those that a mesh axis runs over, the one named last changes fastest.
Arguments:
- queries: bfloat16 [12, 15360, 2560], P('pipe', 'dp'), may hold values from -6 to 6
- key_rows: bfloat16 [12, 15360, 512], P('pipe', 'dp'), may hold values from -6 to 6
- value_rows: bfloat16 [12, 15360, 512], P('pipe', 'dp'), may hold values from -6 to 6
- out_grad: bfloat16 [12, 15360, 2560], P('pipe', 'dp'), may hold values from -6 to 6
- log_norm: bfloat16 [12, 20, 15360], P('pipe', None, 'dp'), may hold values from 2.5 to 4.5
- row_delta: bfloat16 [12, 20, 15360], P('pipe', None, 'dp'), may hold values from -24 to 24
- cand_lengths: int32 [12, 64, 3], P('pipe', 'dp'), may hold values from 0 to 80, as said below
Outputs:
- up_q: bfloat16 [12, 15360, 2560], P('pipe', 'dp')
- up_k: bfloat16 [12, 15360, 512], P('pipe', 'dp')
- up_v: bfloat16 [12, 15360, 512], P('pipe', 'dp')
- bias_grad: float32 [12, 3072], P('pipe', 'dp')
- value_bias_grad: float32 [12, 512], P('pipe', 'dp')
The draws below stay inside these ranges and needn't reach their ends.
Inputs may be any that keep to these rules, and one draw needn't show every extreme that they name: `cand_lengths`: each block's candidates fill its slots from the front, zeros marking empty slots, and the first slot is never empty; nonzero lengths are 64 or more, and the lengths of one block sum to at most 240. For the blocks i and i + 32 of one section, the rows of one block's candidates that end within its first 160 rows plus the rows of the other block's candidates that end beyond them come to at most 160, both ways round.
All inputs are finite; a program needn't handle non-finite values.
Results may differ from the reference program's by a relative error of at most 0.0054.
Values may be sent and summed in bfloat16 or wider, within the bound.
No kernel may reach another device: no remote copies, remote signals or barrier semaphores. Data moves between devices by JAX's collectives and lax.ppermute only.
A program may use at most 32 MiB of HBM per device.

```python
import math
import jax
import jax.numpy as jnp
from jax import lax

HEADS = 20
KV_HEADS = 4
HEAD_DIM = 128
CANDIDATES = 3
LONGEST = 80
SHORTEST = 64
HOME_ROWS = 240
DP_RANKS = 64
SECTIONS = 12
TOKENS = 15360


def draw_cand_lengths(key, part):
    half_ranks = DP_RANKS // 2
    subkeys = jax.random.split(key, 7)
    shape = (SECTIONS, half_ranks, CANDIDATES)
    slot_index = jnp.arange(CANDIDATES, dtype=jnp.int32)
    heavy = jax.random.randint(subkeys[0], shape, SHORTEST, LONGEST + 1)
    dropped = jax.random.randint(subkeys[1], (SECTIONS, half_ranks), 0, 4) == 0
    pick_section = jax.random.randint(subkeys[2], (), 0, SECTIONS)
    pick_pair = jax.random.randint(subkeys[3], (), 0, half_ranks)
    forced = (jnp.arange(SECTIONS)[:, None] == pick_section) & (jnp.arange(half_ranks)[None, :] == pick_pair)
    dropped = dropped & jnp.logical_not(forced)
    heavy = jnp.where(dropped[:, :, None] & (slot_index == CANDIDATES - 1), 0, heavy)
    heavy = jnp.where(forced[:, :, None], LONGEST, heavy)
    light = jax.random.randint(subkeys[4], shape, SHORTEST, LONGEST + 1)
    light = jnp.where(forced[:, :, None] & (slot_index == 0), LONGEST, light)
    two_light = jax.random.randint(subkeys[6], (SECTIONS, half_ranks), 0, 2) == 1
    light_count = jnp.where(dropped & two_light, 2, 1)
    light = jnp.where(slot_index[None, None, :] < light_count[:, :, None], light, 0)
    flipped = jax.random.randint(subkeys[5], (SECTIONS, half_ranks), 0, 2) == 1
    lower_half = jnp.where(flipped[:, :, None], light, heavy)
    upper_half = jnp.where(flipped[:, :, None], heavy, light)
    return jnp.concatenate([lower_half, upper_half], axis=1).astype(jnp.int32)


def steps_of(stream_key, dims, cuts, low, largest):
    loudness = 1.0
    for axis_at, shards_of in cuts:
        heights = jax.random.uniform(jax.random.fold_in(jax.random.fold_in(stream_key, 6), axis_at), (shards_of,), jnp.float32, low / len(cuts), largest / len(cuts))
        loudness = loudness * jnp.repeat(jnp.exp(heights), dims[axis_at] // shards_of).reshape((-1,) + (1,) * (len(dims) - 1 - axis_at))
    return loudness


def noise(own_key, shape, deviation, limit, cuts=(), kind=jnp.bfloat16):
    result = jax.random.normal(own_key, shape, jnp.float32) * deviation
    if len(cuts) > 0:
        result = steps_of(own_key, shape, cuts, -0.22, 0.18) * result
    return jnp.clip(result, min=-limit, max=limit).astype(kind)


def setup_inputs(seed: int = 0) -> dict:
    arg_keys = jax.random.split(jax.random.key(seed), 8)
    queries = noise(arg_keys[0], (SECTIONS, TOKENS, HEADS * HEAD_DIM), 1.0, 6.0, ((0, 12), (1, 64)))
    key_rows = noise(arg_keys[1], (SECTIONS, TOKENS, KV_HEADS * HEAD_DIM), 1.0, 6.0, ((0, 12), (1, 64)))
    value_rows = noise(arg_keys[2], (SECTIONS, TOKENS, KV_HEADS * HEAD_DIM), 1.0, 6.0, ((0, 12), (1, 64)))
    out_grad = noise(arg_keys[3], (SECTIONS, TOKENS, HEADS * HEAD_DIM), 1.0, 6.0, ((0, 12), (1, 64)))
    log_norm = jnp.clip(2.5 + 2.0 * jax.random.uniform(arg_keys[4], (SECTIONS, HEADS, TOKENS), jnp.float32) ** steps_of(arg_keys[4], (SECTIONS, HEADS, TOKENS), ((0, 12), (2, 64)), -0.2, 0.2), 2.5, 4.5).astype(jnp.bfloat16)
    row_delta = noise(arg_keys[5], (SECTIONS, HEADS, TOKENS), 4.0, 24.0, ((0, 12), (2, 64)))
    cand_lengths = draw_cand_lengths(jax.random.fold_in(arg_keys[7], 71), 0)
    return {"queries": queries, "key_rows": key_rows, "value_rows": value_rows, "out_grad": out_grad, "log_norm": log_norm, "row_delta": row_delta, "cand_lengths": cand_lengths}


def segment_mask(lengths, row_count):
    row_ends = jnp.cumsum(lengths)
    position = jnp.arange(row_count, dtype=jnp.int32)
    labels = lax.optimization_barrier(jnp.sum((position[:, None] >= row_ends[None, :]).astype(jnp.int32), axis=1))
    inside = position < row_ends[-1]
    return (labels[:, None] == labels[None, :]) & inside[:, None] & inside[None, :]

def device_backward(pieces):
    query_part, key_part, value_part, grad_part, norm_part, delta_part, length_part = pieces
    row_count = query_part.shape[0]
    per_group = HEADS // KV_HEADS
    factor = 1.0 / math.sqrt(HEAD_DIM)
    allowed = segment_mask(length_part, row_count)
    query_heads = query_part.reshape(row_count, KV_HEADS, per_group, HEAD_DIM).astype(jnp.float32)
    grad_heads = grad_part.reshape(row_count, KV_HEADS, per_group, HEAD_DIM).astype(jnp.float32)
    key_heads = key_part.reshape(row_count, KV_HEADS, HEAD_DIM).astype(jnp.float32)
    value_heads = value_part.reshape(row_count, KV_HEADS, HEAD_DIM).astype(jnp.float32)
    norm_heads = norm_part.astype(jnp.float32).reshape(KV_HEADS, per_group, row_count)
    delta_heads = delta_part.astype(jnp.float32).reshape(KV_HEADS, per_group, row_count)
    scores = jnp.einsum('ikgd,jkd->kgij', query_heads, key_heads) * factor
    probs = jnp.where(allowed[None, None], jnp.exp(scores - norm_heads[..., None]), 0.0)
    dprobs = jnp.einsum('ikgd,jkd->kgij', grad_heads, value_heads)
    dscores = probs * (dprobs - delta_heads[..., None])
    probs_low = lax.optimization_barrier(probs.astype(jnp.bfloat16)).astype(jnp.float32)
    dscores_low = lax.optimization_barrier(dscores.astype(jnp.bfloat16)).astype(jnp.float32)
    grad_q = (jnp.einsum('kgij,jkd->ikgd', dscores_low, key_heads) * factor).astype(jnp.bfloat16)
    grad_k = (jnp.einsum('kgij,ikgd->jkd', dscores_low, query_heads) * factor).astype(jnp.bfloat16)
    grad_v = jnp.einsum('kgij,ikgd->jkd', probs_low, grad_heads).astype(jnp.bfloat16)
    return (grad_q.reshape(row_count, HEADS * HEAD_DIM), grad_k.reshape(row_count, KV_HEADS * HEAD_DIM), grad_v.reshape(row_count, KV_HEADS * HEAD_DIM))

def reference(queries, key_rows, value_rows, out_grad, log_norm, row_delta, cand_lengths):
    block_count = SECTIONS * DP_RANKS

    def rows_view(tensor):
        return tensor.reshape(block_count, HOME_ROWS, tensor.shape[-1])

    def head_view(tensor):
        split_view = tensor.reshape(SECTIONS, HEADS, DP_RANKS, HOME_ROWS)
        return jnp.moveaxis(split_view, 2, 1).reshape(block_count, HEADS, HOME_ROWS)
    grad_q, grad_k, grad_v = lax.map(device_backward, (rows_view(queries), rows_view(key_rows), rows_view(value_rows), rows_view(out_grad), head_view(log_norm), head_view(row_delta), cand_lengths.reshape(block_count, CANDIDATES)))
    grad_q = grad_q.reshape(SECTIONS, TOKENS, HEADS * HEAD_DIM)
    grad_k = grad_k.reshape(SECTIONS, TOKENS, KV_HEADS * HEAD_DIM)
    grad_v = grad_v.reshape(SECTIONS, TOKENS, KV_HEADS * HEAD_DIM)
    up_q = jnp.roll(grad_q, -1, axis=0)
    up_k = jnp.roll(grad_k, -1, axis=0)
    up_v = jnp.roll(grad_v, -1, axis=0)
    bias_grad = jnp.concatenate([lax.optimization_barrier(jnp.sum(up_q, axis=1, dtype=jnp.float32)), lax.optimization_barrier(jnp.sum(up_k, axis=1, dtype=jnp.float32))], axis=1)
    value_bias_grad = lax.optimization_barrier(jnp.sum(up_v, axis=1, dtype=jnp.float32))
    return (up_q, up_k, up_v, bias_grad, value_bias_grad)
```

```python
import functools
import math

import jax
import jax.numpy as jnp
from jax import lax
from jax.experimental import pallas as pl
from jax.experimental.pallas import tpu as pltpu
from jax.sharding import PartitionSpec as P


HEADS = 20
KV_HEADS = 4
HEAD_DIM = 128
PER_GROUP = HEADS // KV_HEADS
CANDIDATES = 3
LONGEST = 80
HOME_ROWS = 240
PAIR = 2
WIDTH = PER_GROUP * LONGEST
MAIN = WIDTH // 128 * 128
REST = WIDTH - MAIN
CORNER = 256
CHUNK = HOME_ROWS + REST
FACTOR = 1.0 / math.sqrt(HEAD_DIM)
BF16 = jnp.bfloat16
F32 = jnp.float32


def dot(left, right, left_dim=1, right_dim=0):
    return lax.dot_general(
        left, right, (((left_dim,), (right_dim,)), ((), ())), preferred_element_type=F32
    )


def iota(shape, axis):
    return lax.broadcasted_iota(jnp.int32, shape, axis)


def spans(lengths):
    starts = [jnp.zeros_like(lengths[0])]
    for c in range(CANDIDATES - 1):
        starts.append(starts[-1] + lengths[c])
    return starts, lengths


def stored_spans(lengths_ref):
    return spans([lengths_ref[0, c] for c in range(CANDIDATES)])


def sent_spans(ds_ref):
    corner = ds_ref[HOME_ROWS:CHUNK, CORNER:].astype(F32).astype(jnp.int32)
    return spans([corner[c : c + 1, :1] for c in range(CANDIDATES)])


def one_hot(hit):
    return jnp.where(hit, 1.0, 0.0).astype(BF16)


def to_slots(found):
    starts, lengths = found
    shape = (LONGEST, HOME_ROWS)
    row, home = iota(shape, 0), iota(shape, 1)
    return jnp.concatenate(
        [one_hot((home == row + starts[c]) & (row < lengths[c])) for c in range(CANDIDATES)], axis=0
    )


def to_home(found):
    starts, lengths = found
    shape = (HOME_ROWS, HOME_ROWS)
    home, slot = iota(shape, 0), iota(shape, 1)
    hit = jnp.zeros(shape, jnp.bool_)
    for c in range(CANDIDATES):
        j = slot - c * LONGEST
        hit = hit | ((home == j + starts[c]) & (j >= 0) & (j < lengths[c]))
    return one_hot(hit)


def rows_of(tensor, c):
    return tensor[c * LONGEST : (c + 1) * LONGEST]


def stacked(tensor, g, c):
    part = rows_of(tensor, c)
    base = g * PER_GROUP
    return jnp.concatenate(
        [part[:, (base + h) * HEAD_DIM : (base + h + 1) * HEAD_DIM] for h in range(PER_GROUP)], axis=0
    )


def scores_kernel(
    pair, lengths_ref, q_ref, k_ref, v_ref, o_ref, norm_ref, delta_ref, *refs
):
    ds_ref, dkv_ref = refs[-2:]
    found = stored_spans(lengths_ref)
    slots, home = to_slots(found), to_home(found)
    q = dot(slots, q_ref[...]).astype(BF16)
    k = dot(slots, k_ref[...]).astype(BF16)
    v = dot(slots, v_ref[...]).astype(BF16)
    o = dot(slots, o_ref[...]).astype(BF16)
    starts, lengths = found
    shape = (HOME_ROWS, WIDTH)
    at, lane = iota(shape, 0), iota(shape, 1)
    head_of = iota((PER_GROUP, WIDTH), 1)
    own = (head_of >= iota((PER_GROUP, WIDTH), 0) * LONGEST) & (
        head_of < (iota((PER_GROUP, WIDTH), 0) + 1) * LONGEST
    )
    within = lane
    for h in range(1, PER_GROUP):
        within = jnp.where(lane >= h * LONGEST, lane - h * LONGEST, within)
    rest = [[] for _ in range(PAIR)]
    dk = [[] for _ in range(PAIR)]
    dv = [[] for _ in range(PAIR)]
    for c in range(CANDIDATES):
        spread = one_hot((at == within + starts[c]) & (within < lengths[c]))
        norms = dot(norm_ref[...], spread)
        deltas = dot(delta_ref[...], spread)
        for g in range(PAIR):
            base = (pair * PAIR + g) * PER_GROUP
            norm = jnp.sum(jnp.where(own, norms[base : base + PER_GROUP], 0.0), axis=0, keepdims=True)
            delta = jnp.sum(jnp.where(own, deltas[base : base + PER_GROUP], 0.0), axis=0, keepdims=True)
            q_rows, o_rows = stacked(q, g, c), stacked(o, g, c)
            k_part = rows_of(k, c)[:, g * HEAD_DIM : (g + 1) * HEAD_DIM]
            v_part = rows_of(v, c)[:, g * HEAD_DIM : (g + 1) * HEAD_DIM]
            probs = jnp.exp(dot(k_part, q_rows, 1, 1) * FACTOR - norm)
            dscores = probs * (dot(v_part, o_rows, 1, 1) - delta)
            probs_low, dscores_low = probs.astype(BF16), dscores.astype(BF16)
            dk[g].append(dot(dscores_low, q_rows) * FACTOR)
            dv[g].append(dot(probs_low, o_rows))
            ds_ref[g * CHUNK + c * LONGEST : g * CHUNK + (c + 1) * LONGEST, :] = dscores_low[:, :MAIN]
            rest[g].append(dscores[:, MAIN:])
    for g in range(PAIR):
        for at, grads in ((g, dk[g]), (PAIR + g, dv[g])):
            rows = jnp.concatenate(grads, axis=0).astype(BF16)
            dkv_ref[:, at * HEAD_DIM : (at + 1) * HEAD_DIM] = dot(home, rows).astype(BF16)
        turned = jnp.concatenate(rest[g], axis=0).T
        tail = slice(g * CHUNK + HOME_ROWS, (g + 1) * CHUNK)
        ds_ref[tail, :CORNER] = jnp.zeros((REST, CORNER), BF16)
        ds_ref[tail, :HOME_ROWS] = turned.astype(BF16)
        corner = jnp.zeros((REST, MAIN - CORNER), F32)
        for c in range(CANDIDATES):
            corner = jnp.where(iota(corner.shape, 0) == c, lengths[c].astype(F32), corner)
        ds_ref[tail, CORNER:] = corner.astype(BF16)


def query_grads(ds_ref, k, g):
    k_group = k[:, g * HEAD_DIM : (g + 1) * HEAD_DIM]
    turned = ds_ref[g * CHUNK + HOME_ROWS : (g + 1) * CHUNK, :HOME_ROWS]
    lane = iota((REST, HOME_ROWS), 1)
    found = []
    for c in range(CANDIDATES):
        main = dot(
            ds_ref[g * CHUNK + c * LONGEST : g * CHUNK + (c + 1) * LONGEST, :], rows_of(k_group, c), 0, 0
        )
        mine = (lane >= c * LONGEST) & (lane < (c + 1) * LONGEST)
        last = dot(jnp.where(mine, turned.astype(F32), 0.0).astype(BF16), k_group)
        rows = (jnp.concatenate([main, last], axis=0) * FACTOR).astype(BF16)
        found.append(
            jnp.concatenate([rows[h * LONGEST : (h + 1) * LONGEST] for h in range(PER_GROUP)], axis=1)
        )
    return jnp.concatenate(found, axis=0)


def queries_kernel(k_ref, first_ref, second_ref, out_ref):
    found = sent_spans(first_ref)
    k = dot(to_slots(found), k_ref[...]).astype(BF16)
    home = to_home(found)
    width = PER_GROUP * HEAD_DIM
    for pair, ds_ref in enumerate((first_ref, second_ref)):

        @pl.when(pl.program_id(0) == pair)
        def _(ds_ref=ds_ref):
            for g in range(PAIR):
                out_ref[:, g * width : (g + 1) * width] = dot(home, query_grads(ds_ref, k, g)).astype(BF16)


def sums_kernel(lengths_ref, k_ref, first_ref, second_ref, dkv_ref, out_ref):
    k = dot(to_slots(stored_spans(lengths_ref)), k_ref[...]).astype(BF16)
    ranks = out_ref.shape[0] * out_ref.shape[1]

    def total(rows):
        return jnp.sum(rows.astype(F32), axis=0, keepdims=True)

    sums = []
    for pair, ds_ref in enumerate((first_ref, second_ref)):
        part = k[:, pair * PAIR * HEAD_DIM : (pair + 1) * PAIR * HEAD_DIM]
        sums += [total(query_grads(ds_ref, part, g)) for g in range(PAIR)]
    both = total(dkv_ref[...])
    parts = [both[:, at * KW : (at + 1) * KW] for at in range(2 * KV_HEADS // PAIR)]
    sums = jnp.concatenate(sums + parts[0::2], axis=1)
    value_sums = jnp.concatenate(parts[1::2], axis=1)
    step, value_step = sums.shape[1] // ranks, value_sums.shape[1] // ranks

    def folded(row, width):
        return jnp.concatenate([row[:, i * width : (i + 1) * width] for i in range(8)], axis=0)

    sums = folded(sums, 8 * step)
    pad = jnp.zeros((8, 128 - 8 * value_step), F32)
    value_sums = jnp.concatenate([folded(value_sums, 8 * value_step), pad], axis=1)
    lane = iota((8, 128), 1)
    for p in range(8):
        left = pltpu.roll(sums, (sums.shape[1] - step * p) % sums.shape[1], 1)[:, :128]
        right = pltpu.roll(value_sums, (step - value_step * p) % 128, 1)
        out_ref[:, p, :] = jnp.where(
            lane < step, left, jnp.where(lane < step + value_step, right, 0.0)
        )


def last_kernel(dkv_ref, sums_ref, k_ref, v_ref, bias_ref, value_bias_ref):
    for pair in range(KV_HEADS // PAIR):
        k_ref[:, pair * KW : (pair + 1) * KW] = dkv_ref[:, 2 * pair * KW : (2 * pair + 1) * KW]
        v_ref[:, pair * KW : (pair + 1) * KW] = dkv_ref[:, (2 * pair + 1) * KW : (2 * pair + 2) * KW]
    step = bias_ref.shape[1]
    bias_ref[...] = sums_ref[:, :step]
    value_bias_ref[...] = sums_ref[:, step : step + value_bias_ref.shape[1]]


VMEM_LIMIT = 67_043_328
SMEM = pl.BlockSpec(memory_space=pltpu.SMEM)


def whole(shape):
    return pl.BlockSpec(shape, lambda i: (0,) * len(shape))


def columns(width, at):
    return pl.BlockSpec((HOME_ROWS, width), lambda i: (0, at))


QW = PAIR * PER_GROUP * HEAD_DIM
KW = PAIR * HEAD_DIM


def kernel(body, flops, moved, exps=0, steps=1, **rest):
    return pl.pallas_call(
        body,
        grid=(steps,),
        cost_estimate=pl.CostEstimate(flops=flops, bytes_accessed=moved, transcendentals=exps),
        compiler_params=pltpu.CompilerParams(vmem_limit_bytes=VMEM_LIMIT),
        **rest,
    )


def score_grads(pair, lengths, q, k, v, o, norm, delta, earlier):
    shape = jax.ShapeDtypeStruct
    extra = () if earlier is None else (earlier,)
    return kernel(
        functools.partial(scores_kernel, pair),
        800_000_000,
        2_400_000,
        400_000,
        out_shape=(shape((PAIR * CHUNK, MAIN), BF16), shape((HOME_ROWS, 2 * KV_HEADS * HEAD_DIM), BF16)),
        in_specs=[
            SMEM,
            columns(QW, pair),
            columns(KW, pair),
            columns(KW, pair),
            columns(QW, pair),
            whole((HEADS, HOME_ROWS)),
            whole((HEADS, HOME_ROWS)),
        ]
        + [pl.BlockSpec(memory_space=pl.ANY)] * len(extra),
        out_specs=(whole((PAIR * CHUNK, MAIN)), columns(2 * KW, pair)),
        input_output_aliases={7: 1} if extra else {},
    )(lengths, q, k, v, o, norm, delta, *extra)


def query_out(k, ds):
    return kernel(
        queries_kernel,
        600_000_000,
        2_400_000,
        steps=KV_HEADS // PAIR,
        out_shape=jax.ShapeDtypeStruct((HOME_ROWS, HEADS * HEAD_DIM), BF16),
        in_specs=[pl.BlockSpec((HOME_ROWS, KW), lambda i: (0, i))] + [whole((PAIR * CHUNK, MAIN))] * 2,
        out_specs=pl.BlockSpec((HOME_ROWS, QW), lambda i: (0, i)),
    )(k, *ds)


def column_sums(ranks, lengths, k, ds, dkv):
    return kernel(
        sums_kernel,
        300_000_000,
        2_000_000,
        out_shape=jax.ShapeDtypeStruct((8, ranks // 8, 128), F32),
        in_specs=[SMEM, whole((HOME_ROWS, KV_HEADS * HEAD_DIM))]
        + [whole((PAIR * CHUNK, MAIN))] * 2
        + [whole((HOME_ROWS, 2 * KV_HEADS * HEAD_DIM))],
        out_specs=whole((8, ranks // 8, 128)),
    )(lengths, k, *ds, dkv)


def arrived(ranks, dkv, sums):
    shape = jax.ShapeDtypeStruct
    wide = KV_HEADS * HEAD_DIM
    small = ((HEADS + KV_HEADS) * HEAD_DIM // ranks, wide // ranks)
    return kernel(
        last_kernel,
        0,
        1_000_000,
        out_shape=(shape((HOME_ROWS, wide), BF16),) * 2 + tuple(shape((1, n), F32) for n in small),
        in_specs=[whole((HOME_ROWS, 2 * wide)), whole((1, 128))],
        out_specs=(whole((HOME_ROWS, wide)),) * 2 + tuple(whole((1, n)) for n in small),
    )(dkv, sums)


def up(value):
    count = lax.axis_size("pipe")
    return lax.ppermute(value, "pipe", [(s, (s - 1) % count) for s in range(count)])


def relay(q, k, v, o, norm, delta, lengths):
    ranks = lax.axis_size("dp")
    k_up = up(k)
    ds, ds_up, dkv = [], [], None
    for pair in range(KV_HEADS // PAIR):
        found, dkv = score_grads(pair, lengths, q, k, v, o, norm, delta, dkv)
        ds.append(found)
        ds_up.append(up(found))
    dkv_up = up(dkv)
    pieces = column_sums(ranks, lengths, k, ds, dkv)
    spread = lax.all_to_all(pieces.reshape(ranks, 1, 128), "dp", 0, 0, tiled=True)
    sums = up(jnp.sum(spread, axis=0))
    up_q = query_out(k_up, ds_up)
    return (up_q, *arrived(ranks, dkv_up, sums))


def shards(queries, key_rows, value_rows, out_grad, log_norm, row_delta, cand_lengths):
    up_q, up_k, up_v, bias, value_bias = relay(
        queries[0], key_rows[0], value_rows[0], out_grad[0], log_norm[0], row_delta[0], cand_lengths[0]
    )
    return up_q[None], up_k[None], up_v[None], bias, value_bias


def solution(mesh):
    in_specs = (
        P("pipe", "dp", None),
        P("pipe", "dp", None),
        P("pipe", "dp", None),
        P("pipe", "dp", None),
        P("pipe", None, "dp"),
        P("pipe", None, "dp"),
        P("pipe", "dp", None),
    )
    out_specs = (
        P("pipe", "dp", None),
        P("pipe", "dp", None),
        P("pipe", "dp", None),
        P("pipe", "dp"),
        P("pipe", "dp"),
    )
    return jax.shard_map(shards, mesh=mesh, in_specs=in_specs, out_specs=out_specs, check_vma=False)
```

```python
import functools
import math

import jax
import jax.numpy as jnp
from jax import lax
from jax.experimental import pallas as pl
from jax.experimental.pallas import tpu as pltpu
from jax.sharding import PartitionSpec as P


HEADS = 20
KV_HEADS = 4
HEAD_DIM = 128
PER_GROUP = HEADS // KV_HEADS
CANDIDATES = 3
LONGEST = 80
HOME_ROWS = 240
PAIR = 2
WIDTH = PER_GROUP * LONGEST
MAIN = WIDTH // 128 * 128
REST = WIDTH - MAIN
CHUNK = HOME_ROWS + REST
TILES = MAIN // 128
FACTOR = 1.0 / math.sqrt(HEAD_DIM)
BF16 = jnp.bfloat16
F32 = jnp.float32


def dot(left, right, left_dim=1, right_dim=0):
    return lax.dot_general(
        left, right, (((left_dim,), (right_dim,)), ((), ())), preferred_element_type=F32
    )


def iota(shape, axis):
    return lax.broadcasted_iota(jnp.int32, shape, axis)


def spans(lengths):
    starts = [jnp.zeros_like(lengths[0])]
    for c in range(CANDIDATES - 1):
        starts.append(starts[-1] + lengths[c])
    return starts, lengths


def stored_spans(lengths_ref):
    return spans([lengths_ref[0, c] for c in range(CANDIDATES)])


SCORE_ROWS = PAIR * TILES * CHUNK
GRAD_ROWS = 2 * PAIR * HOME_ROWS
FIRST = (SCORE_ROWS, 128)
SECOND = (GRAD_ROWS + SCORE_ROWS + GRAD_ROWS, 128)


def tile(g, m):
    return (g * TILES + m) * CHUNK


def grads_at(at):
    return slice(at * HOME_ROWS, (at + 1) * HOME_ROWS)


def sent_spans(ref):
    start = tile(0, TILES - 1) + HOME_ROWS
    corner = ref[start : start + REST, :].astype(F32).astype(jnp.int32)
    return spans([corner[c : c + 1, :1] for c in range(CANDIDATES)])


def total(rows):
    return jnp.sum(rows.astype(F32), axis=0, keepdims=True)


def one_hot(hit):
    return jnp.where(hit, 1.0, 0.0).astype(BF16)


def to_slots(found):
    starts, lengths = found
    shape = (LONGEST, HOME_ROWS)
    row, home = iota(shape, 0), iota(shape, 1)
    return jnp.concatenate(
        [one_hot((home == row + starts[c]) & (row < lengths[c])) for c in range(CANDIDATES)], axis=0
    )


def to_home(found):
    starts, lengths = found
    shape = (HOME_ROWS, HOME_ROWS)
    home, slot = iota(shape, 0), iota(shape, 1)
    hit = jnp.zeros(shape, jnp.bool_)
    for c in range(CANDIDATES):
        j = slot - c * LONGEST
        hit = hit | ((home == j + starts[c]) & (j >= 0) & (j < lengths[c]))
    return one_hot(hit)


def rows_of(tensor, c):
    return tensor[c * LONGEST : (c + 1) * LONGEST]


def stacked(tensor, g, c):
    part = rows_of(tensor, c)
    base = g * PER_GROUP
    return jnp.concatenate(
        [part[:, (base + h) * HEAD_DIM : (base + h + 1) * HEAD_DIM] for h in range(PER_GROUP)], axis=0
    )


def scores_kernel(
    pair, lengths_ref, q_ref, k_ref, v_ref, o_ref, norm_ref, delta_ref, *refs
):
    if pair == 0:
        earlier_ref, (out_ref, grads_ref, sums_ref) = None, refs
    else:
        earlier_ref, _, both_ref, sums_ref = refs
        out_ref, grads_ref = both_ref.at[:SCORE_ROWS], both_ref.at[SCORE_ROWS:]
    found = stored_spans(lengths_ref)
    slots, home = to_slots(found), to_home(found)
    q = dot(slots, q_ref[...]).astype(BF16)
    k = dot(slots, k_ref[...]).astype(BF16)
    v = dot(slots, v_ref[...]).astype(BF16)
    o = dot(slots, o_ref[...]).astype(BF16)
    starts, lengths = found
    shape = (HOME_ROWS, WIDTH)
    at, lane = iota(shape, 0), iota(shape, 1)
    head_of = iota((PER_GROUP, WIDTH), 1)
    own = (head_of >= iota((PER_GROUP, WIDTH), 0) * LONGEST) & (
        head_of < (iota((PER_GROUP, WIDTH), 0) + 1) * LONGEST
    )
    within = lane
    for h in range(1, PER_GROUP):
        within = jnp.where(lane >= h * LONGEST, lane - h * LONGEST, within)
    head_at, head_lane = iota((WIDTH, 128), 0), iota((WIDTH, 128), 1) * LONGEST
    heads = one_hot((head_at >= head_lane) & (head_at < head_lane + LONGEST))
    per_head = [[] for _ in range(PAIR)]
    rest = [[] for _ in range(PAIR)]
    dk = [[] for _ in range(PAIR)]
    dv = [[] for _ in range(PAIR)]
    for c in range(CANDIDATES):
        spread = one_hot((at == within + starts[c]) & (within < lengths[c]))
        norms = dot(norm_ref[...], spread)
        deltas = dot(delta_ref[...], spread)
        for g in range(PAIR):
            base = (pair * PAIR + g) * PER_GROUP
            norm = jnp.sum(jnp.where(own, norms[base : base + PER_GROUP], 0.0), axis=0, keepdims=True)
            delta = jnp.sum(jnp.where(own, deltas[base : base + PER_GROUP], 0.0), axis=0, keepdims=True)
            q_rows, o_rows = stacked(q, g, c), stacked(o, g, c)
            k_part = rows_of(k, c)[:, g * HEAD_DIM : (g + 1) * HEAD_DIM]
            v_part = rows_of(v, c)[:, g * HEAD_DIM : (g + 1) * HEAD_DIM]
            probs = jnp.exp(dot(k_part, q_rows, 1, 1) * FACTOR - norm)
            dscores = probs * (dot(v_part, o_rows, 1, 1) - delta)
            probs_low, dscores_low = probs.astype(BF16), dscores.astype(BF16)
            dk[g].append(dot(dscores_low, q_rows) * FACTOR)
            dv[g].append(dot(probs_low, o_rows))
            per_head[g].append(dot(dscores_low, heads))
            for m in range(TILES):
                start = tile(g, m) + c * LONGEST
                out_ref[start : start + LONGEST, :] = dscores_low[:, m * 128 : (m + 1) * 128]
            rest[g].append(dscores[:, MAIN:])
    sums = [[], [], []]
    for g in range(PAIR):
        for at, grads in ((g, dk[g]), (PAIR + g, dv[g])):
            rows = dot(home, jnp.concatenate(grads, axis=0).astype(BF16)).astype(BF16)
            grads_ref[grads_at(at), :] = rows
            sums[1 + at // PAIR].append(total(rows))
        scores = jnp.concatenate(per_head[g], axis=0)
        coarse = scores.astype(BF16)
        scores = jnp.concatenate([coarse, (scores - coarse.astype(F32)).astype(BF16)], axis=0)
        keys = k[:, g * HEAD_DIM : (g + 1) * HEAD_DIM]
        queries = dot(scores, jnp.concatenate([keys, keys], axis=0), 0, 0) * FACTOR
        sums[0] += [queries[h : h + 1] for h in range(PER_GROUP)]
        turned = jnp.concatenate(rest[g], axis=0).T.astype(BF16)
        corner = jnp.zeros((REST, 128), F32)
        for c in range(CANDIDATES):
            corner = jnp.where(iota(corner.shape, 0) == c, lengths[c].astype(F32), corner)
        pad = jnp.zeros((REST, (TILES - 1) * 128 - HOME_ROWS), BF16)
        turned = jnp.concatenate([turned, pad, corner.astype(BF16)], axis=1)
        for m in range(TILES):
            start = tile(g, m) + HOME_ROWS
            out_ref[start : start + REST, :] = turned[:, m * 128 : (m + 1) * 128]
    sums = [jnp.concatenate(row, axis=1) for row in sums]
    if earlier_ref is None:
        sums_ref[...] = jnp.concatenate(sums, axis=1)
    else:
        before = earlier_ref[...]
        parts = before[:, :QW], before[:, QW : QW + KW], before[:, QW + KW :]
        both = [row for pair_of in zip(parts, sums) for row in pair_of]
        fill_pieces(sums_ref, jnp.concatenate(both[:4], axis=1), jnp.concatenate(both[4:], axis=1))


def query_grads(ref, g, k_group):
    def lines(start, rows):
        at = [tile(g, m) + start for m in range(TILES)]
        return jnp.concatenate([ref[a : a + rows, :] for a in at], axis=1)

    turned = lines(HOME_ROWS, REST)[:, :HOME_ROWS]
    lane = iota((REST, HOME_ROWS), 1)
    found = []
    for c in range(CANDIDATES):
        main = dot(lines(c * LONGEST, LONGEST), rows_of(k_group, c), 0, 0)
        mine = (lane >= c * LONGEST) & (lane < (c + 1) * LONGEST)
        last = dot(jnp.where(mine, turned.astype(F32), 0.0).astype(BF16), k_group)
        rows = (jnp.concatenate([main, last], axis=0) * FACTOR).astype(BF16)
        found.append(
            jnp.concatenate([rows[h * LONGEST : (h + 1) * LONGEST] for h in range(PER_GROUP)], axis=1)
        )
    return jnp.concatenate(found, axis=0)


def queries_kernel(k_ref, parcel_ref, q_out):
    found = sent_spans(parcel_ref)
    k = dot(to_slots(found), k_ref[...]).astype(BF16)
    home = to_home(found)
    width = PER_GROUP * HEAD_DIM
    for g in range(PAIR):
        rows = query_grads(parcel_ref, g, k[:, g * HEAD_DIM : (g + 1) * HEAD_DIM])
        q_out[:, g * width : (g + 1) * width] = dot(home, rows).astype(BF16)


def last_kernel(k_ref, parcel_ref, spread_ref, _, q_out, k_out, v_out, bias_ref, value_bias_ref):
    queries_kernel(k_ref, parcel_ref.at[GRAD_ROWS : GRAD_ROWS + SCORE_ROWS], q_out)
    for pair in range(KV_HEADS // PAIR):
        grads = parcel_ref.at[pair * (GRAD_ROWS + SCORE_ROWS) : pair * (GRAD_ROWS + SCORE_ROWS) + GRAD_ROWS]
        for g in range(PAIR):
            at = (pair * PAIR + g) * HEAD_DIM
            k_out[:, at : at + HEAD_DIM] = grads[grads_at(g), :]
            v_out[:, at : at + HEAD_DIM] = grads[grads_at(PAIR + g), :]
    sums = total(spread_ref[...])
    step = bias_ref.shape[1]
    bias_ref[...] = sums[:, :step]
    value_bias_ref[...] = sums[:, step : step + value_bias_ref.shape[1]]


def fill_pieces(out_ref, sums, value_sums):
    ranks = out_ref.shape[0] * out_ref.shape[1]
    step, value_step = sums.shape[1] // ranks, value_sums.shape[1] // ranks

    def folded(row, width):
        return jnp.concatenate([row[:, i * width : (i + 1) * width] for i in reversed(range(8))], axis=0)

    sums = folded(sums, 8 * step)
    pad = jnp.zeros((8, 128 - 8 * value_step), F32)
    value_sums = jnp.concatenate([folded(value_sums, 8 * value_step), pad], axis=1)
    lane = iota((8, 128), 1)
    for p in range(8):
        left = pltpu.roll(sums, (sums.shape[1] - step * p) % sums.shape[1], 1)[:, :128]
        right = pltpu.roll(value_sums, (step - value_step * p) % 128, 1)
        out_ref[:, 7 - p, :] = jnp.where(
            lane < step, left, jnp.where(lane < step + value_step, right, 0.0)
        )


VMEM_LIMIT = 67_043_328
SMEM = pl.BlockSpec(memory_space=pltpu.SMEM)


def whole(shape):
    return pl.BlockSpec(shape, lambda i: (0,) * len(shape))


def columns(width, at):
    return pl.BlockSpec((HOME_ROWS, width), lambda i: (0, at))


QW = PAIR * PER_GROUP * HEAD_DIM
KW = PAIR * HEAD_DIM


def kernel(body, flops, moved, exps=0, steps=1, **rest):
    return pl.pallas_call(
        body,
        grid=(steps,),
        cost_estimate=pl.CostEstimate(flops=flops, bytes_accessed=moved, transcendentals=exps),
        compiler_params=pltpu.CompilerParams(vmem_limit_bytes=VMEM_LIMIT),
        **rest,
    )


ANY = pl.BlockSpec(memory_space=pl.ANY)


def score_grads(pair, ranks, lengths, q, k, v, o, norm, delta, earlier):
    shape = jax.ShapeDtypeStruct
    if pair == 0:
        sums = (1, QW + 2 * KW)
        outs = (shape(FIRST, BF16), shape(SECOND, BF16), shape(sums, F32))
        out_specs = (whole(FIRST), pl.BlockSpec((GRAD_ROWS, 128), lambda i: (0, 0)), whole(sums))
        extra, extra_specs, aliases = (), [], {}
    else:
        sums = (8, ranks // 8, 128)
        outs = (shape(SECOND, BF16), shape(sums, F32))
        rows = pl.BlockSpec(
            (pl.Element(SCORE_ROWS + GRAD_ROWS), pl.Element(128)), lambda i: (GRAD_ROWS, 0)
        )
        out_specs = (rows, whole(sums))
        extra, extra_specs, aliases = earlier, [whole(earlier[0].shape), ANY], {8: 0}
    return kernel(
        functools.partial(scores_kernel, pair),
        800_000_000,
        2_400_000,
        400_000,
        out_shape=outs,
        in_specs=[
            SMEM,
            columns(QW, pair),
            columns(KW, pair),
            columns(KW, pair),
            columns(QW, pair),
            whole((HEADS, HOME_ROWS)),
            whole((HEADS, HOME_ROWS)),
        ]
        + extra_specs,
        out_specs=out_specs,
        input_output_aliases=aliases,
    )(lengths, q, k, v, o, norm, delta, *extra)


def first_queries(k, parcel):
    return kernel(
        queries_kernel,
        300_000_000,
        1_600_000,
        out_shape=jax.ShapeDtypeStruct((HOME_ROWS, HEADS * HEAD_DIM), BF16),
        in_specs=[columns(KW, 0), whole(FIRST)],
        out_specs=columns(QW, 0),
    )(k, parcel)


def last_outputs(k, parcel, spread, up_q):
    shape = jax.ShapeDtypeStruct
    wide = KV_HEADS * HEAD_DIM
    ranks = spread.shape[0]
    small = ((HEADS + KV_HEADS) * HEAD_DIM // ranks, wide // ranks)
    return kernel(
        last_kernel,
        300_000_000,
        2_000_000,
        out_shape=(
            (shape((HOME_ROWS, HEADS * HEAD_DIM), BF16),)
            + (shape((HOME_ROWS, wide), BF16),) * 2
            + tuple(shape((1, n), F32) for n in small)
        ),
        in_specs=[columns(KW, 1), whole(SECOND), whole(spread.shape), ANY],
        out_specs=(columns(QW, 1),) + (whole((HOME_ROWS, wide)),) * 2 + tuple(whole((1, n)) for n in small),
        input_output_aliases={3: 0},
    )(k, parcel, spread, up_q)


def up(value):
    count = lax.axis_size("pipe")
    return lax.ppermute(value, "pipe", [(s, (s - 1) % count) for s in range(count)])


def relay(q, k, v, o, norm, delta, lengths):
    ranks = lax.axis_size("dp")
    k_up = up(k)
    first, second, sums = score_grads(0, ranks, lengths, q, k, v, o, norm, delta, None)
    first = up(first)
    second, sums = score_grads(1, ranks, lengths, q, k, v, o, norm, delta, (sums, second))
    sums = up(sums)
    second = up(second)
    backward = [list(reversed(range(ranks)))]
    spread = lax.all_to_all(
        sums.reshape(ranks, 1, 128), "dp", 0, 0, axis_index_groups=backward, tiled=True
    )
    up_q = first_queries(k_up, first)
    return last_outputs(k_up, second, spread.reshape(ranks, 128), up_q)


def shards(queries, key_rows, value_rows, out_grad, log_norm, row_delta, cand_lengths):
    up_q, up_k, up_v, bias, value_bias = relay(
        queries[0], key_rows[0], value_rows[0], out_grad[0], log_norm[0], row_delta[0], cand_lengths[0]
    )
    return up_q[None], up_k[None], up_v[None], bias, value_bias


def solution(mesh):
    in_specs = (
        P("pipe", "dp", None),
        P("pipe", "dp", None),
        P("pipe", "dp", None),
        P("pipe", "dp", None),
        P("pipe", None, "dp"),
        P("pipe", None, "dp"),
        P("pipe", "dp", None),
    )
    out_specs = (
        P("pipe", "dp", None),
        P("pipe", "dp", None),
        P("pipe", "dp", None),
        P("pipe", "dp"),
        P("pipe", "dp"),
    )
    return jax.shard_map(shards, mesh=mesh, in_specs=in_specs, out_specs=out_specs, check_vma=False)
```

```python
import functools
import math

import jax
import jax.numpy as jnp
from jax import lax
from jax.experimental import pallas as pl
from jax.experimental.pallas import tpu as pltpu
from jax.sharding import PartitionSpec as P


HEADS = 20
KV_HEADS = 4
HEAD_DIM = 128
PER_GROUP = HEADS // KV_HEADS
CANDIDATES = 3
LONGEST = 80
HOME_ROWS = 240
PAIR = 2
WIDTH = PER_GROUP * LONGEST
MAIN = WIDTH // 128 * 128
REST = WIDTH - MAIN
CHUNK = HOME_ROWS + REST
TILES = MAIN // 128
FACTOR = 1.0 / math.sqrt(HEAD_DIM)
BF16 = jnp.bfloat16
F32 = jnp.float32


def dot(left, right, left_dim=1, right_dim=0):
    return lax.dot_general(
        left, right, (((left_dim,), (right_dim,)), ((), ())), preferred_element_type=F32
    )


def iota(shape, axis):
    return lax.broadcasted_iota(jnp.int32, shape, axis)


def spans(lengths):
    starts = [jnp.zeros_like(lengths[0])]
    for c in range(CANDIDATES - 1):
        starts.append(starts[-1] + lengths[c])
    return starts, lengths


def stored_spans(lengths_ref):
    return spans([lengths_ref[0, c] for c in range(CANDIDATES)])


SCORE_ROWS = PAIR * TILES * CHUNK
GRAD_ROWS = 2 * PAIR * HOME_ROWS
FIRST = (SCORE_ROWS, 128)
SECOND = (GRAD_ROWS + SCORE_ROWS + GRAD_ROWS, 128)


def tile(g, m):
    return (g * TILES + m) * CHUNK


def grads_at(at):
    return slice(at * HOME_ROWS, (at + 1) * HOME_ROWS)


def sent_spans(ref):
    start = tile(0, TILES - 1) + HOME_ROWS
    corner = ref[start : start + REST, :].astype(F32).astype(jnp.int32)
    return spans([corner[c : c + 1, :1] for c in range(CANDIDATES)])


def total(rows):
    return jnp.sum(rows.astype(F32), axis=0, keepdims=True)


def one_hot(hit):
    return jnp.where(hit, 1.0, 0.0).astype(BF16)


def to_slots(found):
    starts, lengths = found
    shape = (LONGEST, HOME_ROWS)
    row, home = iota(shape, 0), iota(shape, 1)
    return jnp.concatenate(
        [one_hot((home == row + starts[c]) & (row < lengths[c])) for c in range(CANDIDATES)], axis=0
    )


def to_home(found):
    starts, lengths = found
    shape = (HOME_ROWS, HOME_ROWS)
    home, slot = iota(shape, 0), iota(shape, 1)
    hit = jnp.zeros(shape, jnp.bool_)
    for c in range(CANDIDATES):
        j = slot - c * LONGEST
        hit = hit | ((home == j + starts[c]) & (j >= 0) & (j < lengths[c]))
    return one_hot(hit)


def rows_of(tensor, c):
    return tensor[c * LONGEST : (c + 1) * LONGEST]


def stacked(tensor, g, c):
    part = rows_of(tensor, c)
    base = g * PER_GROUP
    return jnp.concatenate(
        [part[:, (base + h) * HEAD_DIM : (base + h + 1) * HEAD_DIM] for h in range(PER_GROUP)], axis=0
    )


def scores_kernel(
    pair, lengths_ref, q_ref, k_ref, v_ref, o_ref, norm_ref, delta_ref, *refs
):
    if pair == 0:
        earlier_ref, (out_ref, grads_ref, sums_ref) = None, refs
    else:
        earlier_ref, _, both_ref, sums_ref = refs
        out_ref, grads_ref = both_ref.at[:SCORE_ROWS], both_ref.at[SCORE_ROWS:]
    found = stored_spans(lengths_ref)
    slots, home = to_slots(found), to_home(found)
    q = dot(slots, q_ref[...]).astype(BF16)
    k = dot(slots, k_ref[...]).astype(BF16)
    v = dot(slots, v_ref[...]).astype(BF16)
    o = dot(slots, o_ref[...]).astype(BF16)
    starts, lengths = found
    shape = (HOME_ROWS, WIDTH)
    at, lane = iota(shape, 0), iota(shape, 1)
    head_of = iota((PER_GROUP, WIDTH), 1)
    own = (head_of >= iota((PER_GROUP, WIDTH), 0) * LONGEST) & (
        head_of < (iota((PER_GROUP, WIDTH), 0) + 1) * LONGEST
    )
    within = lane
    for h in range(1, PER_GROUP):
        within = jnp.where(lane >= h * LONGEST, lane - h * LONGEST, within)
    head_at, head_lane = iota((WIDTH, 128), 0), iota((WIDTH, 128), 1) * LONGEST
    heads = one_hot((head_at >= head_lane) & (head_at < head_lane + LONGEST))
    per_head = [[] for _ in range(PAIR)]
    rest = [[] for _ in range(PAIR)]
    dk = [[] for _ in range(PAIR)]
    dv = [[] for _ in range(PAIR)]
    for c in range(CANDIDATES):
        spread = one_hot((at == within + starts[c]) & (within < lengths[c]))
        norms = dot(norm_ref[...], spread)
        deltas = dot(delta_ref[...], spread)
        for g in range(PAIR):
            base = (pair * PAIR + g) * PER_GROUP
            norm = jnp.sum(jnp.where(own, norms[base : base + PER_GROUP], 0.0), axis=0, keepdims=True)
            delta = jnp.sum(jnp.where(own, deltas[base : base + PER_GROUP], 0.0), axis=0, keepdims=True)
            q_rows, o_rows = stacked(q, g, c), stacked(o, g, c)
            k_part = rows_of(k, c)[:, g * HEAD_DIM : (g + 1) * HEAD_DIM]
            v_part = rows_of(v, c)[:, g * HEAD_DIM : (g + 1) * HEAD_DIM]
            probs = jnp.exp(dot(k_part, q_rows, 1, 1) * FACTOR - norm)
            dscores = probs * (dot(v_part, o_rows, 1, 1) - delta)
            probs_low, dscores_low = probs.astype(BF16), dscores.astype(BF16)
            dk[g].append(dot(dscores_low, q_rows) * FACTOR)
            dv[g].append(dot(probs_low, o_rows))
            per_head[g].append(dot(dscores_low, heads))
            for m in range(TILES):
                start = tile(g, m) + c * LONGEST
                out_ref[start : start + LONGEST, :] = dscores_low[:, m * 128 : (m + 1) * 128]
            rest[g].append(dscores[:, MAIN:])
    sums = [[], [], []]
    for g in range(PAIR):
        for at, grads in ((g, dk[g]), (PAIR + g, dv[g])):
            rows = dot(home, jnp.concatenate(grads, axis=0).astype(BF16)).astype(BF16)
            grads_ref[grads_at(at), :] = rows
            sums[1 + at // PAIR].append(total(rows))
        scores = jnp.concatenate(per_head[g], axis=0)
        coarse = scores.astype(BF16)
        scores = jnp.concatenate([coarse, (scores - coarse.astype(F32)).astype(BF16)], axis=0)
        keys = k[:, g * HEAD_DIM : (g + 1) * HEAD_DIM]
        queries = dot(scores, jnp.concatenate([keys, keys], axis=0), 0, 0) * FACTOR
        sums[0] += [queries[h : h + 1] for h in range(PER_GROUP)]
        turned = jnp.concatenate(rest[g], axis=0).T.astype(BF16)
        corner = jnp.zeros((REST, 128), F32)
        for c in range(CANDIDATES):
            corner = jnp.where(iota(corner.shape, 0) == c, lengths[c].astype(F32), corner)
        pad = jnp.zeros((REST, (TILES - 1) * 128 - HOME_ROWS), BF16)
        turned = jnp.concatenate([turned, pad, corner.astype(BF16)], axis=1)
        for m in range(TILES):
            start = tile(g, m) + HOME_ROWS
            out_ref[start : start + REST, :] = turned[:, m * 128 : (m + 1) * 128]
    sums = [jnp.concatenate(row, axis=1) for row in sums]
    if earlier_ref is None:
        sums_ref[...] = jnp.concatenate(sums, axis=1)
    else:
        before = earlier_ref[...]
        parts = before[:, :QW], before[:, QW : QW + KW], before[:, QW + KW :]
        both = [row for pair_of in zip(parts, sums) for row in pair_of]
        fill_pieces(sums_ref, jnp.concatenate(both[:4], axis=1), jnp.concatenate(both[4:], axis=1))


def query_grads(ref, g, k_group):
    def lines(start, rows):
        at = [tile(g, m) + start for m in range(TILES)]
        return jnp.concatenate([ref[a : a + rows, :] for a in at], axis=1)

    turned = lines(HOME_ROWS, REST)[:, :HOME_ROWS]
    lane = iota((REST, HOME_ROWS), 1)
    found = []
    for c in range(CANDIDATES):
        main = dot(lines(c * LONGEST, LONGEST), rows_of(k_group, c), 0, 0)
        mine = (lane >= c * LONGEST) & (lane < (c + 1) * LONGEST)
        last = dot(jnp.where(mine, turned.astype(F32), 0.0).astype(BF16), k_group)
        rows = (jnp.concatenate([main, last], axis=0) * FACTOR).astype(BF16)
        found.append(
            jnp.concatenate([rows[h * LONGEST : (h + 1) * LONGEST] for h in range(PER_GROUP)], axis=1)
        )
    return jnp.concatenate(found, axis=0)


def queries_kernel(k_ref, parcel_ref, q_out):
    found = sent_spans(parcel_ref)
    k = dot(to_slots(found), k_ref[...]).astype(BF16)
    home = to_home(found)
    width = PER_GROUP * HEAD_DIM
    for g in range(PAIR):
        rows = query_grads(parcel_ref, g, k[:, g * HEAD_DIM : (g + 1) * HEAD_DIM])
        q_out[:, g * width : (g + 1) * width] = dot(home, rows).astype(BF16)


def last_kernel(k_ref, parcel_ref, spread_ref, _, q_out, k_out, v_out, bias_ref, value_bias_ref):
    queries_kernel(k_ref, parcel_ref.at[GRAD_ROWS : GRAD_ROWS + SCORE_ROWS], q_out)
    for pair in range(KV_HEADS // PAIR):
        grads = parcel_ref.at[pair * (GRAD_ROWS + SCORE_ROWS) : pair * (GRAD_ROWS + SCORE_ROWS) + GRAD_ROWS]
        for g in range(PAIR):
            at = (pair * PAIR + g) * HEAD_DIM
            k_out[:, at : at + HEAD_DIM] = grads[grads_at(g), :]
            v_out[:, at : at + HEAD_DIM] = grads[grads_at(PAIR + g), :]
    sums = total(spread_ref[...])
    step = bias_ref.shape[1]
    bias_ref[...] = sums[:, :step]
    value_bias_ref[...] = sums[:, step : step + value_bias_ref.shape[1]]


def fill_pieces(out_ref, sums, value_sums):
    ranks = out_ref.shape[0] * out_ref.shape[1]
    step, value_step = sums.shape[1] // ranks, value_sums.shape[1] // ranks

    def folded(row, width):
        return jnp.concatenate([row[:, i * width : (i + 1) * width] for i in reversed(range(8))], axis=0)

    sums = folded(sums, 8 * step)
    pad = jnp.zeros((8, 128 - 8 * value_step), F32)
    value_sums = jnp.concatenate([folded(value_sums, 8 * value_step), pad], axis=1)
    lane = iota((8, 128), 1)
    for p in range(8):
        left = pltpu.roll(sums, (sums.shape[1] - step * p) % sums.shape[1], 1)[:, :128]
        right = pltpu.roll(value_sums, (step - value_step * p) % 128, 1)
        out_ref[:, 7 - p, :] = jnp.where(
            lane < step, left, jnp.where(lane < step + value_step, right, 0.0)
        )


SOME_VMEM = 24 * 2**20
SMEM = pl.BlockSpec(memory_space=pltpu.SMEM)


def whole(shape):
    return pl.BlockSpec(shape, lambda i: (0,) * len(shape))


def columns(width, at):
    return pl.BlockSpec((HOME_ROWS, width), lambda i: (0, at))


QW = PAIR * PER_GROUP * HEAD_DIM
KW = PAIR * HEAD_DIM


def kernel(body, limit, flops, moved, exps=0, **rest):
    return pl.pallas_call(
        body,
        grid=(1,),
        cost_estimate=pl.CostEstimate(flops=flops, bytes_accessed=moved, transcendentals=exps),
        compiler_params=pltpu.CompilerParams(vmem_limit_bytes=limit),
        **rest,
    )


ANY = pl.BlockSpec(memory_space=pl.ANY)


def score_grads(pair, ranks, lengths, q, k, v, o, norm, delta, earlier):
    shape = jax.ShapeDtypeStruct
    if pair == 0:
        sums = (1, QW + 2 * KW)
        outs = (shape(FIRST, BF16), shape(SECOND, BF16), shape(sums, F32))
        out_specs = (whole(FIRST), pl.BlockSpec((GRAD_ROWS, 128), lambda i: (0, 0)), whole(sums))
        extra, extra_specs, aliases = (), [], {}
    else:
        sums = (8, ranks // 8, 128)
        outs = (shape(SECOND, BF16), shape(sums, F32))
        rows = pl.BlockSpec(
            (pl.Element(SCORE_ROWS + GRAD_ROWS), pl.Element(128)), lambda i: (GRAD_ROWS, 0)
        )
        out_specs = (rows, whole(sums))
        extra, extra_specs, aliases = earlier, [whole(earlier[0].shape), ANY], {8: 0}
    return kernel(
        functools.partial(scores_kernel, pair),
        (60 * 2**20, 24 * 2**20)[pair],
        800_000_000,
        2_400_000,
        400_000,
        out_shape=outs,
        in_specs=[
            SMEM,
            columns(QW, pair),
            columns(KW, pair),
            columns(KW, pair),
            columns(QW, pair),
            whole((HEADS, HOME_ROWS)),
            whole((HEADS, HOME_ROWS)),
        ]
        + extra_specs,
        out_specs=out_specs,
        input_output_aliases=aliases,
    )(lengths, q, k, v, o, norm, delta, *extra)


def first_queries(k, parcel):
    return kernel(
        queries_kernel,
        SOME_VMEM,
        300_000_000,
        1_600_000,
        out_shape=jax.ShapeDtypeStruct((HOME_ROWS, HEADS * HEAD_DIM), BF16),
        in_specs=[columns(KW, 0), whole(FIRST)],
        out_specs=columns(QW, 0),
    )(k, parcel)


def last_outputs(k, parcel, spread, up_q):
    shape = jax.ShapeDtypeStruct
    wide = KV_HEADS * HEAD_DIM
    ranks = spread.shape[0]
    small = ((HEADS + KV_HEADS) * HEAD_DIM // ranks, wide // ranks)
    return kernel(
        last_kernel,
        SOME_VMEM,
        300_000_000,
        2_000_000,
        out_shape=(
            (shape((HOME_ROWS, HEADS * HEAD_DIM), BF16),)
            + (shape((HOME_ROWS, wide), BF16),) * 2
            + tuple(shape((1, n), F32) for n in small)
        ),
        in_specs=[columns(KW, 1), whole(SECOND), whole(spread.shape), ANY],
        out_specs=(columns(QW, 1),) + (whole((HOME_ROWS, wide)),) * 2 + tuple(whole((1, n)) for n in small),
        input_output_aliases={3: 0},
    )(k, parcel, spread, up_q)


def up(value):
    count = lax.axis_size("pipe")
    return lax.ppermute(value, "pipe", [(s, (s - 1) % count) for s in range(count)])


def relay(q, k, v, o, norm, delta, lengths):
    ranks = lax.axis_size("dp")
    k_up = up(k)
    first, second, sums = score_grads(0, ranks, lengths, q, k, v, o, norm, delta, None)
    first = up(first)
    second, sums = score_grads(1, ranks, lengths, q, k, v, o, norm, delta, (sums, second))
    sums = up(sums)
    second = up(second)
    backward = [list(reversed(range(ranks)))]
    spread = lax.all_to_all(
        sums.reshape(ranks, 1, 128), "dp", 0, 0, axis_index_groups=backward, tiled=True
    )
    up_q = first_queries(k_up, first)
    return last_outputs(k_up, second, spread.reshape(ranks, 128), up_q)


def shards(queries, key_rows, value_rows, out_grad, log_norm, row_delta, cand_lengths):
    up_q, up_k, up_v, bias, value_bias = relay(
        queries[0], key_rows[0], value_rows[0], out_grad[0], log_norm[0], row_delta[0], cand_lengths[0]
    )
    return up_q[None], up_k[None], up_v[None], bias, value_bias


def solution(mesh):
    in_specs = (
        P("pipe", "dp", None),
        P("pipe", "dp", None),
        P("pipe", "dp", None),
        P("pipe", "dp", None),
        P("pipe", None, "dp"),
        P("pipe", None, "dp"),
        P("pipe", "dp", None),
    )
    out_specs = (
        P("pipe", "dp", None),
        P("pipe", "dp", None),
        P("pipe", "dp", None),
        P("pipe", "dp"),
        P("pipe", "dp"),
    )
    return jax.shard_map(shards, mesh=mesh, in_specs=in_specs, out_specs=out_specs, check_vma=False)
```
